32 devices in a mesh: view: 8 (over z, core), head: 4 (over y, x).
Axes of the slice: x: 2, y: 2, z: 4, core: 2. Of those that a mesh axis runs over, the one named last changes fastest.
Arguments:
- tokens: bfloat16 [16, 512, 1024], P('view', 'head'), may hold values from -6 to 6
- w_qkv_frame: bfloat16 [1024, 3072], replicated, may hold values from -2 to 2
- w_out_frame: bfloat16 [1024, 1024], replicated, may hold values from -0.1875 to 0.1875
- w_qkv_global: bfloat16 [1024, 3072], replicated, may hold values from -2 to 2
- w_out_global: bfloat16 [1024, 1024], replicated, may hold values from -0.1875 to 0.1875
Outputs:
- result: bfloat16 [16, 512, 1024], P('view', 'head')
The draws below stay inside these ranges and needn't reach their ends.
All inputs are finite; a program needn't handle non-finite values.
Results may differ from the reference program's by a relative error of at most 0.012.
Values may be sent and summed in bfloat16 or wider, within the bound.
A program may use at most 128 MiB of HBM per device.

```python
import math
import jax
import jax.numpy as jnp
from jax import lax

D = 1024
HEADS = 16
HEAD = 64
TOK = 512
VIEWS = 16


def qkv_table(key):
    column_scale = 1.7 / math.sqrt(D)
    key_query = jax.random.fold_in(key, 0)
    table = jax.random.normal(key_query, (D, 3 * D), jnp.float32) * column_scale
    return jnp.clip(table, -2.0, 2.0).astype(jnp.bfloat16)


def draw_w_qkv_frame(key, part):
    return qkv_table(jax.random.fold_in(key, 11))


def draw_w_qkv_global(key, part):
    return qkv_table(jax.random.fold_in(key, 23))


def steps_of(key, extent, cuts, least, largest):
    factor_of, own = 1.0, jax.random.fold_in(key, 6)
    for position, parts in cuts:
        heights = jnp.exp(jax.random.uniform(jax.random.fold_in(own, position), (parts,), jnp.float32, least / len(cuts), largest / len(cuts)))
        factor_of = factor_of * jnp.repeat(heights, extent[position] // parts).reshape([-1 if axis == position else 1 for axis in range(len(extent))])
    return factor_of


def normal_values(stream_key, extent, deviation, reach, pieces=(), held_as=jnp.bfloat16):
    array = deviation * jax.random.normal(stream_key, extent, jnp.float32)
    if pieces:
        array = array * steps_of(stream_key, extent, pieces, -0.22, 0.18)
    return jnp.clip(array, -reach, reach).astype(held_as)


def setup_inputs(seed: int = 0) -> dict:
    keys = jax.random.split(jax.random.key(seed), 6)
    return {
        "tokens": normal_values(keys[0], (VIEWS, TOK, D), 1.0, 6.0, ((0, 8), (1, 4))),
        "w_qkv_frame": draw_w_qkv_frame(jax.random.fold_in(keys[5], 71), 0),
        "w_out_frame": normal_values(keys[2], (D, D), D ** -0.5, 0.1875),
        "w_qkv_global": draw_w_qkv_global(jax.random.fold_in(keys[5], 71), 0),
        "w_out_global": normal_values(keys[4], (D, D), D ** -0.5, 0.1875),
    }


def normalize(stream):
    widened = stream.astype(jnp.float32)
    center = lax.optimization_barrier(jnp.mean(widened, axis=-1, keepdims=True))
    spread = lax.optimization_barrier(jnp.mean(jnp.square(widened - center), axis=-1, keepdims=True))
    return ((widened - center) * lax.rsqrt(spread + 1e-06)).astype(jnp.bfloat16)

def project_qkv(stream, weight):
    normed = normalize(stream).reshape(VIEWS * TOK, D)
    packed = jnp.dot(normed, weight, preferred_element_type=jnp.float32).astype(jnp.bfloat16)
    return packed.reshape(VIEWS * TOK, 3, HEADS, HEAD)

def attend(queries, keys_all, values_all):
    scores = jnp.dot(queries, keys_all.T, preferred_element_type=jnp.float32) * HEAD ** (-0.5)
    top_score = lax.optimization_barrier(jnp.max(scores, axis=-1, keepdims=True))
    exp_terms = jnp.exp(scores - top_score)
    row_sum = lax.optimization_barrier(jnp.sum(exp_terms, axis=-1, keepdims=True))
    shares = exp_terms.astype(jnp.bfloat16)
    return jnp.dot(shares, values_all, preferred_element_type=jnp.float32) / row_sum

def frame_view(packed):
    mixed_out = jax.vmap(attend, in_axes=(1, 1, 1), out_axes=1)(packed[:, 0], packed[:, 1], packed[:, 2])
    return mixed_out.astype(jnp.bfloat16).reshape(TOK, D)

def reference(tokens, w_qkv_frame, w_out_frame, w_qkv_global, w_out_global):
    packed_frame = project_qkv(tokens, w_qkv_frame).reshape(VIEWS, TOK, 3, HEADS, HEAD)
    frame_mixed = lax.map(frame_view, packed_frame)
    added_frame = jnp.dot(frame_mixed.reshape(VIEWS * TOK, D), w_out_frame, preferred_element_type=jnp.float32)
    after_frame = (tokens.astype(jnp.float32) + added_frame.reshape(VIEWS, TOK, D)).astype(jnp.bfloat16)
    packed_global = project_qkv(after_frame, w_qkv_global)

    def one_head(head_id):
        query_head = packed_global[:, 0, head_id]
        key_head = packed_global[:, 1, head_id]
        value_head = packed_global[:, 2, head_id]
        blocks_out = lax.map(lambda qblock: attend(qblock, key_head, value_head).astype(jnp.bfloat16), query_head.reshape(VIEWS, TOK, HEAD))
        return blocks_out
    per_head = lax.map(one_head, jnp.arange(HEADS, dtype=jnp.int32))
    global_mixed = jnp.transpose(per_head, (1, 2, 0, 3)).reshape(VIEWS * TOK, D)
    added_global = jnp.dot(global_mixed, w_out_global, preferred_element_type=jnp.float32)
    return (after_frame.astype(jnp.float32) + added_global.reshape(VIEWS, TOK, D)).astype(jnp.bfloat16)
```

```python
import functools
import math

import jax
import jax.numpy as jnp
from jax import lax
from jax.experimental import pallas as pl
from jax.experimental.pallas import tpu as pltpu
from jax.sharding import PartitionSpec as P

HEAD = 64
LANES = 128
CORES = 2
SUM_ROWS = 16
KEY_STEP = 512
SCORE_SCALE = HEAD ** (-0.5) * math.log2(math.e)
VMEM_BYTES = 56 * 2**20


def normalize(stream):
    widened = stream.astype(jnp.float32)
    center = jnp.mean(widened, axis=-1, keepdims=True)
    spread = jnp.mean(jnp.square(widened - center), axis=-1, keepdims=True)
    return ((widened - center) * lax.rsqrt(spread + 1e-06)).astype(jnp.bfloat16)


def arrive(ref, sem):
    pltpu.make_async_copy(ref, ref, sem).wait()


def block_kernel(
    planes, copies,
    tokens_ref, w_qkv_frame_ref, w_out_frame_ref, w_qkv_global_ref, w_out_global_ref,
    out_ref,
    raw, normed, w_frame, w_back, w_global, w_out, packed_frame,
    mixed_buf, mixed_in, after_buf, after_own, packed,
    got_q, got_kv, keys, values, peaks, accums, out_buf, out_back,
    w_frame_sem, w_back_sem, w_global_sem, w_out_sem,
    token_send, token_recv, relay_send, mixed_send, mixed_recv, after_send, after_recv,
    q_send, q_recv, kv_send, kv_recv, on_send, on_recv, out_send, out_recv,
):
    views_here, rows, model_dim = tokens_ref.shape
    view, spot = lax.axis_index("view"), lax.axis_index("head")
    spots, view_size = lax.axis_size("head"), lax.axis_size("view")
    heads, _, head, width = packed.shape
    pairs = mixed_buf.shape[1]
    cols = w_frame.shape[2]
    chunk = w_global.shape[2]
    per_plane = heads // planes
    group = spots // (CORES * views_here)
    shares = CORES * group

    core, row = lax.rem(view, CORES), view // CORES
    mine = spot // group
    share = lax.rem(spot, group) * CORES + core
    first_core, first_local = mine // views_here, lax.rem(mine, views_here)

    plane, copy = view // copies, lax.rem(view, copies)
    my_head = plane * per_plane + spot
    stage_rows = per_plane * width

    def remote(src, dst, send, recv, target):
        return pltpu.make_async_remote_copy(
            src_ref=src, dst_ref=dst, send_sem=send, recv_sem=recv,
            device_id=target, device_id_type=pl.DeviceIdType.MESH,
        )

    def either(here, far, near):
        @pl.when(here)
        def _():
            near().start()

        @pl.when(jnp.logical_not(here))
        def _():
            far().start()

    def left(here, far, near):
        @pl.when(jnp.logical_not(here))
        def _():
            far().wait_send()

    def frame_weight(which):
        at = pl.multiple_of(which * model_dim + share * cols, LANES)
        return pltpu.make_async_copy(
            w_qkv_frame_ref.at[:, pl.ds(at, cols)], w_frame.at[which], w_frame_sem.at[which]
        )

    def global_weight(i):
        return pltpu.make_async_copy(
            w_qkv_global_ref.at[:, i * chunk : (i + 1) * chunk], w_global.at[i],
            w_global_sem.at[i],
        )

    def back_weight():
        return pltpu.make_async_copy(w_out_frame_ref, w_back, w_back_sem)

    def out_weight():
        return pltpu.make_async_copy(w_out_global_ref, w_out, w_out_sem)

    def token_copy(i, k):
        to_spot = (core * views_here + i) * group + k
        src, dst, landed = tokens_ref.at[i], raw.at[spot], token_recv.at[spot]
        far = lambda: remote(src, dst, token_send.at[i, k], landed, (view, to_spot))
        return to_spot == spot, far, lambda: pltpu.make_async_copy(src, dst, landed)

    def relay_copy(source):
        return remote(
            raw.at[source], raw.at[source], relay_send.at[source], token_recv.at[source],
            (row * CORES + (CORES - 1 - core), spot),
        )

    def mixed_copy(pair, step):
        to_share = lax.rem(share + step, shares)
        return remote(
            mixed_buf.at[to_share, pair], mixed_in.at[share, pair],
            mixed_send.at[pair, step], mixed_recv.at[pair, share],
            (row * CORES + lax.rem(to_share, CORES), mine * group + to_share // CORES),
        )

    def mixed_own(pair):
        return pltpu.make_async_copy(
            mixed_buf.at[share, pair], mixed_in.at[share, pair], mixed_recv.at[pair, share]
        )

    def after_copy(t):
        to_view, to_spot = row * CORES + first_core, share * views_here + t
        here = jnp.logical_and(to_view == view, to_spot == spot)
        src, dst, landed = after_buf.at[t], after_own.at[first_local], after_recv.at[first_local]
        far = lambda: remote(src, dst, after_send.at[t], landed, (to_view, to_spot))
        return here, far, lambda: pltpu.make_async_copy(src, dst, landed)

    def device(to_plane, to_spot):
        return (to_plane * copies + copy, to_spot)

    def q_copy(stage, step):
        to_plane, to_spot = lax.rem(plane + stage, planes), lax.rem(spot + step, per_plane)
        slot, order = stage * per_plane + spot, stage * per_plane + step
        return remote(
            packed.at[to_plane * per_plane + to_spot, 0], got_q.at[slot],
            q_send.at[order], q_recv.at[slot], device(to_plane, to_spot),
        )

    def kv_copy(stage, step):
        to_plane, to_spot = lax.rem(plane + stage, planes), lax.rem(spot + step, per_plane)
        slot, order = stage * per_plane + spot, stage * per_plane + step
        return remote(
            packed.at[to_plane * per_plane + to_spot, pl.ds(1, 2)], got_kv.at[0, slot],
            kv_send.at[order], kv_recv.at[slot], device(to_plane, to_spot),
        )

    def on_copy(slot, hop):
        return remote(
            got_kv.at[0, slot], got_kv.at[hop, slot], on_send.at[hop - 1, slot],
            on_recv.at[hop - 1, slot],
            (plane * copies + lax.rem(copy + hop, copies), spot),
        )

    def back_copy(block, i, t):
        slot = block * per_plane + i
        from_view = lax.rem(plane + planes - block, planes) * copies + copy
        from_row, from_core = from_view // CORES, lax.rem(from_view, CORES)
        its_view, its_share = i // group, (i % group) * CORES + from_core
        to_view = from_row * CORES + its_view // views_here
        to_spot = its_share * views_here + t
        here = jnp.logical_and(to_view == view, to_spot == spot)
        src, dst = out_buf.at[slot, t], out_back.at[my_head, its_view % views_here]
        landed = out_recv.at[my_head, its_view % views_here]
        far = lambda: remote(src, dst, out_send.at[slot, t], landed, (to_view, to_spot))
        return here, far, lambda: pltpu.make_async_copy(src, dst, landed)

    for which in range(3):
        frame_weight(which).start()

    barrier = pltpu.get_barrier_semaphore()

    def greet(i, carry):
        pl.semaphore_signal(
            barrier, inc=1,
            device_id=(lax.rem(view + i // spots, view_size), lax.rem(spot + lax.rem(i, spots), spots)),
            device_id_type=pl.DeviceIdType.MESH,
        )
        return carry

    lax.fori_loop(1, view_size * spots, greet, 0)
    pl.semaphore_wait(barrier, view_size * spots - 1)

    for i in range(views_here):
        for k in range(group):
            either(*token_copy(i, k))
    back_weight().start()
    for i in range(w_global.shape[0]):
        global_weight(i).start()
    out_weight().start()
    peaks[...] = jnp.full_like(peaks, -1e30)
    accums[...] = jnp.zeros_like(accums)
    values[head:, :] = jnp.ones((SUM_ROWS, values.shape[1]), jnp.bfloat16)

    def take(step, carry):
        source = lax.rem(spot + step, spots)
        arrive(raw.at[source], token_recv.at[source])

        @pl.when(first_core == core)
        def _():
            relay_copy(source).start()

        at = pl.ds(pl.multiple_of(source * rows, rows), rows)
        normed[at, :] = normalize(raw[source])
        return carry

    lax.fori_loop(0, spots, take, 0)
    for which in range(3):
        frame_weight(which).wait()
        part = jnp.dot(normed[...], w_frame[which], preferred_element_type=jnp.float32)
        if which == 0:
            part = part * SCORE_SCALE
        packed_frame[which] = part.astype(jnp.bfloat16)

    view_rows = spots * rows
    low = lax.broadcasted_iota(jnp.int32, (view_rows, LANES), 1) < HEAD
    for pair in range(pairs):
        at = slice(pair * LANES, (pair + 1) * LANES)
        queries, its_keys, its_values = (packed_frame[which, :, at] for which in range(3))
        outs = []
        for mask in (low, jnp.logical_not(low)):
            scores = lax.dot_general(
                queries, jnp.where(mask, its_keys, 0), (((1,), (1,)), ((), ())),
                preferred_element_type=jnp.float32,
            )
            terms = jnp.exp2(scores - jnp.max(scores, axis=1, keepdims=True))
            outs.append(
                jnp.dot(
                    terms.astype(jnp.bfloat16), jnp.where(mask, its_values, 1),
                    preferred_element_type=jnp.float32,
                )
            )
        total = jnp.where(low, outs[0][:, LANES - 1 :], outs[1][:, :1])
        mixed = (jnp.where(low, outs[0], outs[1]) / total).astype(jnp.bfloat16)
        for j in range(shares):
            mixed_buf[j, pair] = mixed[j * width : (j + 1) * width]
        for step in range(1, shares):
            mixed_copy(pair, step).start()
        mixed_own(pair).start()

    for pair in range(pairs):
        for j in range(shares):
            arrive(mixed_in.at[j, pair], mixed_recv.at[pair, j])
    gathered = jnp.concatenate(
        [mixed_in[j, pair] for j in range(shares) for pair in range(pairs)], axis=1
    )
    back_weight().wait()
    added = jnp.dot(gathered, w_back[...], preferred_element_type=jnp.float32)
    stream = raw[pl.ds(share * views_here, views_here)].reshape(width, model_dim)
    after = (stream.astype(jnp.float32) + added).astype(jnp.bfloat16)
    after_buf[...] = after.reshape(views_here, rows, model_dim)
    normed[:width, :] = normalize(after)

    def project(which, stage):
        to_plane = lax.rem(plane + stage, planes)
        part = jnp.dot(
            normed[:width, :], w_global[which * planes + to_plane],
            preferred_element_type=jnp.float32,
        )
        if which == 0:
            part = part * SCORE_SCALE
        part = part.astype(jnp.bfloat16).T
        for i in range(per_plane):
            packed[to_plane * per_plane + i, which] = part[i * head : (i + 1) * head]

    def start_stage(make, stage):
        for step in range(per_plane):
            make(stage, step).start()

    def nth(i):
        odd = lax.rem(i, 2)
        return odd * ((i + 1) // 2) + (1 - odd) * lax.rem(planes - i // 2, planes)

    for i in range(w_global.shape[0]):
        global_weight(i).wait()

    def project_queries(i, carry):
        stage = nth(i)
        project(0, stage)
        start_stage(q_copy, stage)
        return carry

    def project_rest(i, carry):
        project(1, nth(i))
        project(2, nth(i))
        return carry

    lax.fori_loop(1, planes, project_queries, 0)
    project(1, 0)
    project(2, 0)
    for step in range(1, per_plane):
        kv_copy(0, step).start()
    pltpu.make_async_copy(
        packed.at[my_head, pl.ds(1, 2)], got_kv.at[0, spot], kv_recv.at[spot]
    ).start()
    project(0, 0)
    for step in range(1, per_plane):
        q_copy(0, step).start()
    pltpu.make_async_copy(packed.at[my_head, 0], got_q.at[spot], q_recv.at[spot]).start()
    lax.fori_loop(1, planes, project_rest, 0)
    for t in range(views_here):
        either(*after_copy(t))

    def hand_on(stage):
        for i in range(per_plane):
            slot = stage * per_plane + i
            arrive(got_kv.at[0, slot], kv_recv.at[slot])
            for hop in range(1, copies):
                on_copy(slot, hop).start()

    def send_back(block):
        for i in range(per_plane):
            for t in range(views_here):
                either(*back_copy(block, i, t))

    hand_on(0)

    def step_fn(step, carry):
        turn, nth_stage = lax.rem(step, planes), step // planes
        stage = nth(nth_stage)
        last = (nth_stage + 1) // planes
        block = nth(turn + last * (planes - 1 - 2 * turn))

        @pl.when(turn == 0)
        def _():
            for hop in range(1, copies):
                for i in range(per_plane):
                    slot = stage * per_plane + i
                    arrive(got_kv.at[hop, slot], on_recv.at[hop - 1, slot])
            for hop in range(copies):
                for i in range(per_plane):
                    slot = stage * per_plane + i
                    at = (hop * per_plane + i) * width
                    keys[at : at + width, :] = got_kv[hop, slot, 0].T
                    values[:head, at : at + width] = got_kv[hop, slot, 1]

        @pl.when(nth_stage == 0)
        def _():
            for i in range(per_plane):
                slot = block * per_plane + i
                arrive(got_q.at[slot], q_recv.at[slot])

        @pl.when(jnp.logical_and(lax.rem(step, 2) == 0, step // 2 + 1 < planes))
        def _():
            start_stage(kv_copy, nth(step // 2 + 1))

        @pl.when(jnp.logical_and(turn == planes - 1, last == 0))
        def _():
            hand_on(nth(nth_stage + 1))

        queries = jnp.concatenate(
            [got_q[block * per_plane + i] for i in range(per_plane)], axis=1
        )
        peak, accum = peaks[block], accums[block]
        key_rows = keys.shape[0]
        key_step = min(KEY_STEP, key_rows)

        def score(start):
            return jnp.dot(
                keys[start : start + key_step, :], queries, preferred_element_type=jnp.float32
            )

        scores = score(0)
        for start in range(0, key_rows, key_step):
            following = score(start + key_step) if start + key_step < key_rows else None
            peak_new = jnp.maximum(peak, jnp.max(scores, axis=0, keepdims=True))
            terms = jnp.exp2(scores - peak_new).astype(jnp.bfloat16)
            accum = accum * jnp.exp2(peak - peak_new) + jnp.dot(
                values[:, start : start + key_step], terms, preferred_element_type=jnp.float32
            )
            peak, scores = peak_new, following
        peaks[block] = peak
        accums[block] = accum

        @pl.when(last == 1)
        def _():
            total = accums[block]
            mixed = (total[:head] / total[head : head + 1]).astype(jnp.bfloat16)
            for i in range(per_plane):
                for t in range(views_here):
                    at = i * width + t * rows
                    out_buf[block * per_plane + i, t] = mixed[:, at : at + rows]
            send_back(block)

        return carry

    lax.fori_loop(0, planes * planes, step_fn, 0)

    for i in range(views_here):
        for k in range(group):
            left(*token_copy(i, k))

    @pl.when(first_core == core)
    def _():
        for source in range(spots):
            relay_copy(source).wait_send()

    for pair in range(pairs):
        for step in range(1, shares):
            mixed_copy(pair, step).wait_send()
    for t in range(views_here):
        left(*after_copy(t))

    for stage in range(planes):
        for step in range(per_plane):
            if stage or step:
                q_copy(stage, step).wait_send()
                kv_copy(stage, step).wait_send()
    for slot in range(heads):
        for hop in range(1, copies):
            on_copy(slot, hop).wait_send()

    out_weight().wait()
    for i in range(views_here):
        arrive(after_own.at[i], after_recv.at[i])
        for slot in range(heads):
            arrive(out_back.at[slot, i], out_recv.at[slot, i])
    mixed = jnp.concatenate(
        [out_back[:, i].reshape(heads * head, rows) for i in range(views_here)], axis=1
    )
    added = lax.dot_general(
        mixed, w_out[...], (((0,), (0,)), ((), ())), preferred_element_type=jnp.float32
    )
    stream = after_own[...].reshape(width, model_dim).astype(jnp.float32)
    out_ref[...] = (stream + added).astype(jnp.bfloat16).reshape(views_here, rows, model_dim)

    for block in range(planes):
        for i in range(per_plane):
            for t in range(views_here):
                left(*back_copy(block, i, t))


def on_device(tokens, w_qkv_frame, w_out_frame, w_qkv_global, w_out_global):
    views_here, rows, model_dim = tokens.shape
    spots, view_size = lax.axis_size("head"), lax.axis_size("view")
    heads = model_dim // HEAD
    copies = view_size * spots // heads
    planes = view_size // copies
    group = spots // (CORES * views_here)
    shares = CORES * group
    cols = model_dim // shares
    pairs = cols // LANES
    width = views_here * rows
    per_plane = heads // planes
    stage_rows = per_plane * width
    hops = max(1, copies - 1)
    dma = pltpu.SemaphoreType.DMA
    vmem = lambda *shape: pltpu.VMEM(shape, jnp.bfloat16)
    flops = 4 * heads * view_size * spots * width * width * HEAD
    return pl.pallas_call(
        functools.partial(block_kernel, planes, copies),
        in_specs=[pl.BlockSpec(memory_space=pl.ANY)] * 5,
        out_specs=pl.BlockSpec(memory_space=pltpu.VMEM),
        out_shape=jax.ShapeDtypeStruct(tokens.shape, jnp.bfloat16),
        scratch_shapes=[
            vmem(spots, rows, model_dim),
            vmem(spots * rows, model_dim),
            vmem(3, model_dim, cols),
            vmem(model_dim, model_dim),
            vmem(3 * planes, model_dim, per_plane * HEAD),
            vmem(model_dim, model_dim),
            vmem(3, spots * rows, cols),
            vmem(shares, pairs, width, LANES),
            vmem(shares, pairs, width, LANES),
            vmem(views_here, rows, model_dim),
            vmem(views_here, rows, model_dim),
            vmem(heads, 3, HEAD, width),
            vmem(heads, HEAD, width),
            vmem(copies, heads, 2, HEAD, width),
            vmem(copies * stage_rows, HEAD),
            vmem(HEAD + SUM_ROWS, copies * stage_rows),
            pltpu.VMEM((planes, 1, stage_rows), jnp.float32),
            pltpu.VMEM((planes, HEAD + SUM_ROWS, stage_rows), jnp.float32),
            vmem(heads, views_here, HEAD, rows),
            vmem(heads, views_here, HEAD, rows),
            dma((3,)), dma, dma((3 * planes,)), dma,
            dma((views_here, group)), dma((spots,)), dma((spots,)),
            dma((pairs, shares)), dma((pairs, shares)), dma((views_here,)), dma((views_here,)),
            dma((heads,)), dma((heads,)), dma((heads,)), dma((heads,)),
            dma((hops, heads)), dma((hops, heads)),
            dma((heads, views_here)), dma((heads, views_here)),
        ],
        compiler_params=pltpu.CompilerParams(
            collective_id=0, has_side_effects=True, vmem_limit_bytes=VMEM_BYTES
        ),
        cost_estimate=pl.CostEstimate(flops=flops, bytes_accessed=0, transcendentals=0),
        name="frame_and_global",
    )(tokens, w_qkv_frame, w_out_frame, w_qkv_global, w_out_global)


def solution(mesh):
    return jax.shard_map(
        on_device,
        mesh=mesh,
        in_specs=(P("view", "head", None), P(), P(), P(), P()),
        out_specs=P("view", "head", None),
        check_vma=False,
    )
```

```python
import functools
import math

import jax
import jax.numpy as jnp
from jax import lax
from jax.experimental import pallas as pl
from jax.experimental.pallas import tpu as pltpu
from jax.sharding import PartitionSpec as P

HEAD = 64
LANES = 128
CORES = 2
SUM_ROWS = 16
KEY_STEP = 512
SCORE_SCALE = HEAD ** (-0.5) * math.log2(math.e)
VMEM_BYTES = 56 * 2**20


def normalize(stream):
    widened = stream.astype(jnp.float32)
    center = jnp.mean(widened, axis=-1, keepdims=True)
    spread = jnp.mean(jnp.square(widened - center), axis=-1, keepdims=True)
    return ((widened - center) * lax.rsqrt(spread + 1e-06)).astype(jnp.bfloat16)


def arrive(ref, sem):
    pltpu.make_async_copy(ref, ref, sem).wait()


def block_kernel(
    planes, copies,
    tokens_ref, w_qkv_frame_ref, w_out_frame_ref, w_qkv_global_ref, w_out_global_ref,
    out_ref,
    raw, normed, w_frame, w_back, w_global, w_out, frame_q, frame_k, frame_v,
    mixed_buf, mixed_in, after_buf, after_own, packed,
    got_q, got_kv, keys, values, peaks, accums, out_buf, out_back,
    w_frame_sem, w_back_sem, w_global_sem, w_out_sem,
    token_send, token_recv, relay_send, mixed_send, mixed_recv, after_send, after_recv,
    q_send, q_recv, kv_send, kv_recv, on_send, on_recv, out_send, out_recv,
):
    views_here, rows, model_dim = tokens_ref.shape
    view, spot = lax.axis_index("view"), lax.axis_index("head")
    spots, view_size = lax.axis_size("head"), lax.axis_size("view")
    heads, _, head, width = packed.shape
    pairs = mixed_buf.shape[1] // 2
    cols = w_frame.shape[2]
    chunk = w_global.shape[2]
    per_plane = heads // planes
    group = spots // (CORES * views_here)
    shares = CORES * group

    core, row = lax.rem(view, CORES), view // CORES
    mine = spot // group
    share = lax.rem(spot, group) * CORES + core
    first_core, first_local = mine // views_here, lax.rem(mine, views_here)

    plane, copy = view // copies, lax.rem(view, copies)
    my_head = plane * per_plane + spot
    merge = 1 + (planes + 1) % 2
    turns = planes // merge

    def remote(src, dst, send, recv, target):
        return pltpu.make_async_remote_copy(
            src_ref=src, dst_ref=dst, send_sem=send, recv_sem=recv,
            device_id=target, device_id_type=pl.DeviceIdType.MESH,
        )

    def either(here, far, near):
        @pl.when(here)
        def _():
            near().start()

        @pl.when(jnp.logical_not(here))
        def _():
            far().start()

    def left(here, far, near):
        @pl.when(jnp.logical_not(here))
        def _():
            far().wait_send()

    def frame_weight(which):
        at = pl.multiple_of(which * model_dim + share * cols, LANES)
        return pltpu.make_async_copy(
            w_qkv_frame_ref.at[:, pl.ds(at, cols)], w_frame.at[which], w_frame_sem.at[which]
        )

    def global_weight(i):
        return pltpu.make_async_copy(
            w_qkv_global_ref.at[:, i * chunk : (i + 1) * chunk], w_global.at[i],
            w_global_sem.at[i],
        )

    def back_weight():
        return pltpu.make_async_copy(w_out_frame_ref, w_back, w_back_sem)

    def out_weight():
        return pltpu.make_async_copy(w_out_global_ref, w_out, w_out_sem)

    def token_copy(i, k):
        to_spot = (core * views_here + i) * group + k
        src, dst, landed = tokens_ref.at[i], raw.at[spot], token_recv.at[spot]
        far = lambda: remote(src, dst, token_send.at[i, k], landed, (view, to_spot))
        return to_spot == spot, far, lambda: pltpu.make_async_copy(src, dst, landed)

    def relay_copy(source):
        return remote(
            raw.at[source], raw.at[source], relay_send.at[source], token_recv.at[source],
            (row * CORES + (CORES - 1 - core), spot),
        )

    def mixed_copy(pair, step):
        to_share = lax.rem(share + step, shares)
        return remote(
            mixed_buf.at[to_share, pl.ds(2 * pair, 2)], mixed_in.at[share, pl.ds(2 * pair, 2)],
            mixed_send.at[pair, step], mixed_recv.at[pair, share],
            (row * CORES + lax.rem(to_share, CORES), mine * group + to_share // CORES),
        )

    def mixed_own(pair):
        return pltpu.make_async_copy(
            mixed_buf.at[share, pl.ds(2 * pair, 2)], mixed_in.at[share, pl.ds(2 * pair, 2)],
            mixed_recv.at[pair, share],
        )

    def after_copy(t):
        to_view, to_spot = row * CORES + first_core, share * views_here + t
        here = jnp.logical_and(to_view == view, to_spot == spot)
        src, dst, landed = after_buf.at[t], after_own.at[first_local], after_recv.at[first_local]
        far = lambda: remote(src, dst, after_send.at[t], landed, (to_view, to_spot))
        return here, far, lambda: pltpu.make_async_copy(src, dst, landed)

    def device(to_plane, to_spot):
        return (to_plane * copies + copy, to_spot)

    def q_copy(stage, step):
        to_plane, to_spot = lax.rem(plane + stage, planes), lax.rem(spot + step, per_plane)
        slot, order = stage * per_plane + spot, stage * per_plane + step
        return remote(
            packed.at[to_plane * per_plane + to_spot, 0], got_q.at[slot],
            q_send.at[order], q_recv.at[slot], device(to_plane, to_spot),
        )

    def kv_copy(stage, step):
        to_plane, to_spot = lax.rem(plane + stage, planes), lax.rem(spot + step, per_plane)
        slot, order = stage * per_plane + spot, stage * per_plane + step
        return remote(
            packed.at[to_plane * per_plane + to_spot, pl.ds(1, 2)], got_kv.at[0, slot],
            kv_send.at[order], kv_recv.at[slot], device(to_plane, to_spot),
        )

    def on_copy(slot, hop):
        return remote(
            got_kv.at[0, slot], got_kv.at[hop, slot], on_send.at[hop - 1, slot],
            on_recv.at[hop - 1, slot],
            (plane * copies + lax.rem(copy + hop, copies), spot),
        )

    def back_copy(block, i, t):
        slot = block * per_plane + i
        from_view = lax.rem(plane + planes - block, planes) * copies + copy
        from_row, from_core = from_view // CORES, lax.rem(from_view, CORES)
        its_view, its_share = i // group, (i % group) * CORES + from_core
        to_view = from_row * CORES + its_view // views_here
        to_spot = its_share * views_here + t
        here = jnp.logical_and(to_view == view, to_spot == spot)
        src, dst = out_buf.at[slot, t], out_back.at[my_head, its_view % views_here]
        landed = out_recv.at[my_head, its_view % views_here]
        far = lambda: remote(src, dst, out_send.at[slot, t], landed, (to_view, to_spot))
        return here, far, lambda: pltpu.make_async_copy(src, dst, landed)

    for which in range(3):
        frame_weight(which).start()

    barrier = pltpu.get_barrier_semaphore()

    def greet(i, carry):
        pl.semaphore_signal(
            barrier, inc=1,
            device_id=(lax.rem(view + i // spots, view_size), lax.rem(spot + lax.rem(i, spots), spots)),
            device_id_type=pl.DeviceIdType.MESH,
        )
        return carry

    lax.fori_loop(1, view_size * spots, greet, 0)
    pl.semaphore_wait(barrier, view_size * spots - 1)

    for i in range(views_here):
        for k in range(group):
            either(*token_copy(i, k))
    back_weight().start()
    for i in range(w_global.shape[0]):
        global_weight(i).start()
    out_weight().start()
    peaks[...] = jnp.full_like(peaks, -1e30)
    accums[...] = jnp.zeros_like(accums)
    values[:, head:, :] = jnp.ones((planes, SUM_ROWS, values.shape[2]), jnp.bfloat16)

    def take(step, carry):
        source = lax.rem(spot + step, spots)
        arrive(raw.at[source], token_recv.at[source])

        @pl.when(first_core == core)
        def _():
            relay_copy(source).start()

        at = pl.ds(pl.multiple_of(source * rows, rows), rows)
        normed[at, :] = normalize(raw[source])
        return carry

    lax.fori_loop(0, spots, take, 0)
    for which in range(3):
        frame_weight(which).wait()
        part = jnp.dot(normed[...], w_frame[which], preferred_element_type=jnp.float32)
        if which == 0:
            frame_q[...] = (part * SCORE_SCALE).astype(jnp.bfloat16).T
        elif which == 1:
            frame_k[...] = part.astype(jnp.bfloat16)
        else:
            frame_v[...] = part.astype(jnp.bfloat16).T

    view_rows = spots * rows
    low = lax.broadcasted_iota(jnp.int32, (view_rows, LANES), 1) < head
    ones = jnp.ones((SUM_ROWS, view_rows), jnp.bfloat16)

    def frame_score(i):
        at = slice(i // 2 * LANES, (i // 2 + 1) * LANES)
        mask = jnp.logical_not(low) if i % 2 else low
        return jnp.dot(
            jnp.where(mask, frame_k[:, at], 0), frame_q[at, :],
            preferred_element_type=jnp.float32,
        )

    scores = frame_score(0)
    for i in range(2 * pairs):
        following = frame_score(i + 1) if i + 1 < 2 * pairs else None
        terms = jnp.exp2(scores - jnp.max(scores, axis=0, keepdims=True)).astype(jnp.bfloat16)
        its_values = jnp.concatenate([frame_v[i * head : (i + 1) * head, :], ones], axis=0)
        total = jnp.dot(its_values, terms, preferred_element_type=jnp.float32)
        mixed = (total[:head] / total[head : head + 1]).astype(jnp.bfloat16)
        for j in range(shares):
            mixed_buf[j, i] = mixed[:, j * width : (j + 1) * width]
        scores = following
        if i % 2:
            for step in range(1, shares):
                mixed_copy(i // 2, step).start()
            mixed_own(i // 2).start()

    for pair in range(pairs):
        for j in range(shares):
            arrive(mixed_in.at[j, pl.ds(2 * pair, 2)], mixed_recv.at[pair, j])
    gathered = mixed_in[...].reshape(model_dim, width)
    back_weight().wait()
    added = lax.dot_general(
        gathered, w_back[...], (((0,), (0,)), ((), ())), preferred_element_type=jnp.float32
    )
    stream = raw[pl.ds(share * views_here, views_here)].reshape(width, model_dim)
    after = (stream.astype(jnp.float32) + added).astype(jnp.bfloat16)
    after_buf[...] = after.reshape(views_here, rows, model_dim)
    normed[:width, :] = normalize(after)

    def project(which, stage):
        to_plane = lax.rem(plane + stage, planes)
        part = jnp.dot(
            normed[:width, :], w_global[which * planes + to_plane],
            preferred_element_type=jnp.float32,
        )
        if which == 0:
            part = part * SCORE_SCALE
        part = part.astype(jnp.bfloat16).T
        for i in range(per_plane):
            packed[to_plane * per_plane + i, which] = part[i * head : (i + 1) * head]

    def start_stage(make, stage):
        for step in range(per_plane):
            make(stage, step).start()

    def nth(i):
        odd = lax.rem(i, 2)
        return odd * ((i + 1) // 2) + (1 - odd) * lax.rem(planes - i // 2, planes)

    for i in range(w_global.shape[0]):
        global_weight(i).wait()

    def project_keys(i, carry):
        project(1, nth(i))
        project(2, nth(i))
        return carry

    def project_queries(i, carry):
        project(0, nth(i))
        return carry

    project_queries(1, 0)
    start_stage(q_copy, nth(1))
    project_keys(0, 0)
    for step in range(1, per_plane):
        kv_copy(0, step).start()
    pltpu.make_async_copy(
        packed.at[my_head, pl.ds(1, 2)], got_kv.at[0, spot], kv_recv.at[spot]
    ).start()
    project_queries(0, 0)
    for step in range(1, per_plane):
        q_copy(0, step).start()
    pltpu.make_async_copy(packed.at[my_head, 0], got_q.at[spot], q_recv.at[spot]).start()
    project_keys(1, 0)
    start_stage(kv_copy, nth(1))
    lax.fori_loop(2, planes, project_queries, 0)
    lax.fori_loop(2, planes, project_keys, 0)
    for t in range(views_here):
        either(*after_copy(t))

    def hand_on(stage):
        for i in range(per_plane):
            slot = stage * per_plane + i
            arrive(got_kv.at[0, slot], kv_recv.at[slot])
            for hop in range(1, copies):
                on_copy(slot, hop).start()

    def send_back(block):
        for i in range(per_plane):
            for t in range(views_here):
                either(*back_copy(block, i, t))

    hand_on(0)

    def step_fn(step, carry):
        early = step < 2 * turns
        nth_stage = jnp.where(early, lax.rem(step, 2), step // turns)
        last = (nth_stage + 1) // planes
        turn = jnp.where(early, step // 2, lax.rem(step, turns))
        turn = jnp.where(
            jnp.logical_and(last == 1, jnp.logical_not(early)), turns - 1 - turn, turn
        )
        first = jnp.where(early, turn == 0, lax.rem(step, turns) == 0)
        stage = nth(nth_stage)
        blocks = [nth(turn * merge + m) for m in range(merge)]

        @pl.when(step + 2 < planes)
        def _():
            start_stage(q_copy, nth(step + 2))

        @pl.when(jnp.logical_and(step >= 2, step < planes))
        def _():
            start_stage(kv_copy, nth(step))

        @pl.when(first)
        def _():
            for hop in range(1, copies):
                for i in range(per_plane):
                    slot = stage * per_plane + i
                    arrive(got_kv.at[hop, slot], on_recv.at[hop - 1, slot])
            for hop in range(copies):
                for i in range(per_plane):
                    slot = stage * per_plane + i
                    at = (hop * per_plane + i) * width
                    keys[stage, at : at + width, :] = got_kv[hop, slot, 0].T
                    values[stage, :head, at : at + width] = got_kv[hop, slot, 1]

        @pl.when(nth_stage == 0)
        def _():
            for block in blocks:
                for i in range(per_plane):
                    slot = block * per_plane + i
                    arrive(got_q.at[slot], q_recv.at[slot])

        coming = (step + 1) // turns

        @pl.when(
            jnp.logical_and(
                lax.rem(step + 1, turns) == 0, jnp.logical_and(coming >= 2, coming < planes)
            )
        )
        def _():
            hand_on(nth(coming))

        queries = jnp.concatenate(
            [got_q[block * per_plane + i] for block in blocks for i in range(per_plane)], axis=1
        )
        peak, accum = peaks[turn], accums[turn]
        key_rows = keys.shape[1]
        key_step = min(KEY_STEP, key_rows)

        def score(start):
            return jnp.dot(
                keys[stage, start : start + key_step, :], queries,
                preferred_element_type=jnp.float32,
            )

        scores = score(0)
        for start in range(0, key_rows, key_step):
            following = score(start + key_step) if start + key_step < key_rows else None
            peak_new = jnp.maximum(peak, jnp.max(scores, axis=0, keepdims=True))
            terms = jnp.exp2(scores - peak_new).astype(jnp.bfloat16)
            accum = accum * jnp.exp2(peak - peak_new) + jnp.dot(
                values[stage, :, start : start + key_step], terms,
                preferred_element_type=jnp.float32,
            )
            peak, scores = peak_new, following
        peaks[turn] = peak
        accums[turn] = accum

        @pl.when(step == 0)
        def _():
            hand_on(nth(1))

        @pl.when(last == 1)
        def _():
            total = accums[turn]
            mixed = (total[:head] / total[head : head + 1]).astype(jnp.bfloat16)
            for m, block in enumerate(blocks):
                for i in range(per_plane):
                    for t in range(views_here):
                        at = (m * per_plane + i) * width + t * rows
                        out_buf[block * per_plane + i, t] = mixed[:, at : at + rows]
            for block in reversed(blocks):
                send_back(block)

        return carry

    lax.fori_loop(0, planes * turns, step_fn, 0)

    for i in range(views_here):
        for k in range(group):
            left(*token_copy(i, k))

    @pl.when(first_core == core)
    def _():
        for source in range(spots):
            relay_copy(source).wait_send()

    for pair in range(pairs):
        for step in range(1, shares):
            mixed_copy(pair, step).wait_send()
    for t in range(views_here):
        left(*after_copy(t))

    for stage in range(planes):
        for step in range(per_plane):
            if stage or step:
                q_copy(stage, step).wait_send()
                kv_copy(stage, step).wait_send()
    for slot in range(heads):
        for hop in range(1, copies):
            on_copy(slot, hop).wait_send()

    out_weight().wait()
    for i in range(views_here):
        arrive(after_own.at[i], after_recv.at[i])
        for slot in range(heads):
            arrive(out_back.at[slot, i], out_recv.at[slot, i])
    mixed = jnp.concatenate(
        [out_back[:, i].reshape(heads * head, rows) for i in range(views_here)], axis=1
    )
    added = lax.dot_general(
        mixed, w_out[...], (((0,), (0,)), ((), ())), preferred_element_type=jnp.float32
    )
    stream = after_own[...].reshape(width, model_dim).astype(jnp.float32)
    out_ref[...] = (stream + added).astype(jnp.bfloat16).reshape(views_here, rows, model_dim)

    for block in range(planes):
        for i in range(per_plane):
            for t in range(views_here):
                left(*back_copy(block, i, t))


def on_device(tokens, w_qkv_frame, w_out_frame, w_qkv_global, w_out_global):
    views_here, rows, model_dim = tokens.shape
    spots, view_size = lax.axis_size("head"), lax.axis_size("view")
    heads = model_dim // HEAD
    copies = view_size * spots // heads
    planes = view_size // copies
    group = spots // (CORES * views_here)
    shares = CORES * group
    cols = model_dim // shares
    pairs = cols // LANES
    width = views_here * rows
    per_plane = heads // planes
    stage_rows = per_plane * width
    hops = max(1, copies - 1)
    merge = 1 + (planes + 1) % 2
    turns = planes // merge
    dma = pltpu.SemaphoreType.DMA
    vmem = lambda *shape: pltpu.VMEM(shape, jnp.bfloat16)
    flops = 4 * heads * view_size * spots * width * width * HEAD
    return pl.pallas_call(
        functools.partial(block_kernel, planes, copies),
        in_specs=[pl.BlockSpec(memory_space=pl.ANY)] * 5,
        out_specs=pl.BlockSpec(memory_space=pltpu.VMEM),
        out_shape=jax.ShapeDtypeStruct(tokens.shape, jnp.bfloat16),
        scratch_shapes=[
            vmem(spots, rows, model_dim),
            vmem(spots * rows, model_dim),
            vmem(3, model_dim, cols),
            vmem(model_dim, model_dim),
            vmem(3 * planes, model_dim, per_plane * HEAD),
            vmem(model_dim, model_dim),
            vmem(cols, spots * rows),
            vmem(spots * rows, cols),
            vmem(cols, spots * rows),
            vmem(shares, cols // HEAD, HEAD, width),
            vmem(shares, cols // HEAD, HEAD, width),
            vmem(views_here, rows, model_dim),
            vmem(views_here, rows, model_dim),
            vmem(heads, 3, HEAD, width),
            vmem(heads, HEAD, width),
            vmem(copies, heads, 2, HEAD, width),
            vmem(planes, copies * stage_rows, HEAD),
            vmem(planes, HEAD + SUM_ROWS, copies * stage_rows),
            pltpu.VMEM((turns, 1, merge * stage_rows), jnp.float32),
            pltpu.VMEM((turns, HEAD + SUM_ROWS, merge * stage_rows), jnp.float32),
            vmem(heads, views_here, HEAD, rows),
            vmem(heads, views_here, HEAD, rows),
            dma((3,)), dma, dma((3 * planes,)), dma,
            dma((views_here, group)), dma((spots,)), dma((spots,)),
            dma((pairs, shares)), dma((pairs, shares)), dma((views_here,)), dma((views_here,)),
            dma((heads,)), dma((heads,)), dma((heads,)), dma((heads,)),
            dma((hops, heads)), dma((hops, heads)),
            dma((heads, views_here)), dma((heads, views_here)),
        ],
        compiler_params=pltpu.CompilerParams(
            collective_id=0, has_side_effects=True, vmem_limit_bytes=VMEM_BYTES
        ),
        cost_estimate=pl.CostEstimate(flops=flops, bytes_accessed=0, transcendentals=0),
        name="frame_and_global",
    )(tokens, w_qkv_frame, w_out_frame, w_qkv_global, w_out_global)


def solution(mesh):
    return jax.shard_map(
        on_device,
        mesh=mesh,
        in_specs=(P("view", "head", None), P(), P(), P(), P()),
        out_specs=P("view", "head", None),
        check_vma=False,
    )
```

```python
import functools
import math

import jax
import jax.numpy as jnp
from jax import lax
from jax.experimental import pallas as pl
from jax.experimental.pallas import tpu as pltpu
from jax.sharding import PartitionSpec as P

HEAD = 64
LANES = 128
CORES = 2
SUM_ROWS = 16
KEY_STEP = 512
SCORE_SCALE = HEAD ** (-0.5) * math.log2(math.e)
VMEM_BYTES = 56 * 2**20


def normalize(stream):
    widened = stream.astype(jnp.float32)
    center = jnp.mean(widened, axis=-1, keepdims=True)
    spread = jnp.mean(jnp.square(widened - center), axis=-1, keepdims=True)
    return ((widened - center) * lax.rsqrt(spread + 1e-06)).astype(jnp.bfloat16)


def arrive(ref, sem):
    pltpu.make_async_copy(ref, ref, sem).wait()


def block_kernel(
    planes, copies,
    tokens_ref, w_qkv_frame_ref, w_out_frame_ref, w_qkv_global_ref, w_out_global_ref,
    out_ref,
    raw, normed, w_frame, w_back, w_global, w_out, frame_q, frame_k, frame_v,
    mixed_buf, mixed_in, after_buf, after_own, packed,
    got_q, got_kv, keys, values, peaks, accums, out_buf, out_back,
    w_frame_sem, w_back_sem, w_global_sem, w_out_sem,
    token_send, token_recv, relay_send, mixed_send, mixed_recv, after_send, after_recv,
    q_send, q_recv, kv_send, kv_recv, on_send, on_recv, out_send, out_recv,
):
    views_here, rows, model_dim = tokens_ref.shape
    view, spot = lax.axis_index("view"), lax.axis_index("head")
    spots, view_size = lax.axis_size("head"), lax.axis_size("view")
    heads, _, head, width = packed.shape
    pairs = mixed_buf.shape[1] // 2
    cols = w_frame.shape[2]
    chunk = w_global.shape[2]
    per_plane = heads // planes
    group = spots // (CORES * views_here)
    shares = CORES * group

    core, row = lax.rem(view, CORES), view // CORES
    mine = spot // group
    share = lax.rem(spot, group) * CORES + core
    first_core, first_local = mine // views_here, lax.rem(mine, views_here)

    plane, copy = view // copies, lax.rem(view, copies)
    my_head = plane * per_plane + spot
    stage_rows = per_plane * width
    half = rows // CORES
    merge = 1 + (planes + 1) % 2
    turns = planes // merge

    def remote(src, dst, send, recv, target):
        return pltpu.make_async_remote_copy(
            src_ref=src, dst_ref=dst, send_sem=send, recv_sem=recv,
            device_id=target, device_id_type=pl.DeviceIdType.MESH,
        )

    def either(here, far, near):
        @pl.when(here)
        def _():
            near().start()

        @pl.when(jnp.logical_not(here))
        def _():
            far().start()

    def left(here, far, near):
        @pl.when(jnp.logical_not(here))
        def _():
            far().wait_send()

    def frame_weight(which):
        at = pl.multiple_of(which * model_dim + share * cols, LANES)
        return pltpu.make_async_copy(
            w_qkv_frame_ref.at[:, pl.ds(at, cols)], w_frame.at[which], w_frame_sem.at[which]
        )

    def global_weight(i):
        return pltpu.make_async_copy(
            w_qkv_global_ref.at[:, i * chunk : (i + 1) * chunk], w_global.at[i],
            w_global_sem.at[i],
        )

    def back_weight():
        return pltpu.make_async_copy(w_out_frame_ref, w_back, w_back_sem)

    def out_weight():
        return pltpu.make_async_copy(w_out_global_ref, w_out, w_out_sem)

    def token_copy(i, k, to_core):
        to_spot = (core * views_here + i) * group + k
        part = pl.ds(to_core * half, half)
        src, dst = tokens_ref.at[i, part], raw.at[spot, part]
        landed = token_recv.at[spot, to_core]
        here = jnp.logical_and(to_spot == spot, core == to_core)
        far = lambda: remote(
            src, dst, token_send.at[i, k, to_core], landed, (row * CORES + to_core, to_spot)
        )
        return here, far, lambda: pltpu.make_async_copy(src, dst, landed)

    def relay_copy(source):
        part = raw.at[source, pl.ds(pl.multiple_of(core * half, half), half)]
        return remote(
            part, part, relay_send.at[source], token_recv.at[source, core],
            (row * CORES + (CORES - 1 - core), spot),
        )

    def mixed_copy(pair, step):
        to_share = lax.rem(share + step, shares)
        return remote(
            mixed_buf.at[to_share, pl.ds(2 * pair, 2)], mixed_in.at[share, pl.ds(2 * pair, 2)],
            mixed_send.at[pair, step], mixed_recv.at[pair, share],
            (row * CORES + lax.rem(to_share, CORES), mine * group + to_share // CORES),
        )

    def mixed_own(pair):
        return pltpu.make_async_copy(
            mixed_buf.at[share, pl.ds(2 * pair, 2)], mixed_in.at[share, pl.ds(2 * pair, 2)],
            mixed_recv.at[pair, share],
        )

    def after_copy(t):
        to_view, to_spot = row * CORES + first_core, share * views_here + t
        here = jnp.logical_and(to_view == view, to_spot == spot)
        src, dst, landed = after_buf.at[t], after_own.at[first_local], after_recv.at[first_local]
        far = lambda: remote(src, dst, after_send.at[t], landed, (to_view, to_spot))
        return here, far, lambda: pltpu.make_async_copy(src, dst, landed)

    def device(to_plane, to_spot):
        return (to_plane * copies + copy, to_spot)

    def q_copy(stage, step):
        to_plane, to_spot = lax.rem(plane + stage, planes), lax.rem(spot + step, per_plane)
        slot, order = stage * per_plane + spot, stage * per_plane + step
        return remote(
            packed.at[to_plane * per_plane + to_spot, 0], got_q.at[slot],
            q_send.at[order], q_recv.at[slot], device(to_plane, to_spot),
        )

    def kv_copy(stage, step):
        to_plane, to_spot = lax.rem(plane + stage, planes), lax.rem(spot + step, per_plane)
        slot, order = stage * per_plane + spot, stage * per_plane + step
        return remote(
            packed.at[to_plane * per_plane + to_spot, pl.ds(1, 2)], got_kv.at[0, slot],
            kv_send.at[order], kv_recv.at[slot], device(to_plane, to_spot),
        )

    def on_copy(slot, hop):
        return remote(
            got_kv.at[0, slot], got_kv.at[hop, slot], on_send.at[hop - 1, slot],
            on_recv.at[hop - 1, slot],
            (plane * copies + lax.rem(copy + hop, copies), spot),
        )

    def back_copy(block, i, t):
        slot = block * per_plane + i
        from_view = lax.rem(plane + planes - block, planes) * copies + copy
        from_row, from_core = from_view // CORES, lax.rem(from_view, CORES)
        its_view, its_share = i // group, (i % group) * CORES + from_core
        to_view = from_row * CORES + its_view // views_here
        to_spot = its_share * views_here + t
        here = jnp.logical_and(to_view == view, to_spot == spot)
        src, dst = out_buf.at[slot, t], out_back.at[my_head, its_view % views_here]
        landed = out_recv.at[my_head, its_view % views_here]
        far = lambda: remote(src, dst, out_send.at[slot, t], landed, (to_view, to_spot))
        return here, far, lambda: pltpu.make_async_copy(src, dst, landed)

    for which in range(3):
        frame_weight(which).start()

    barrier = pltpu.get_barrier_semaphore()

    def greet(i, carry):
        pl.semaphore_signal(
            barrier, inc=1,
            device_id=(lax.rem(view + i // spots, view_size), lax.rem(spot + lax.rem(i, spots), spots)),
            device_id_type=pl.DeviceIdType.MESH,
        )
        return carry

    lax.fori_loop(1, view_size * spots, greet, 0)
    pl.semaphore_wait(barrier, view_size * spots - 1)

    for i in range(views_here):
        for k in range(group):
            for to_core in range(CORES):
                either(*token_copy(i, k, to_core))
    back_weight().start()
    for i in range(w_global.shape[0]):
        global_weight(i).start()
    out_weight().start()
    peaks[...] = jnp.full_like(peaks, -1e30)
    accums[...] = jnp.zeros_like(accums)
    values[:, head:, :] = jnp.ones((planes, SUM_ROWS, values.shape[2]), jnp.bfloat16)

    def take(step, its_core):
        source = lax.rem(spot + step, spots)
        part = pl.ds(pl.multiple_of(its_core * half, half), half)
        arrive(raw.at[source, part], token_recv.at[source, its_core])

        @pl.when(its_core == core)
        def _():
            relay_copy(source).start()

        at = pl.ds(pl.multiple_of(source * rows + its_core * half, half), half)
        normed[at, :] = normalize(raw[source, part])

    def take_both(i, carry):
        take(lax.rem(i, spots), lax.rem(core + i // spots, CORES))
        return carry

    lax.fori_loop(0, CORES * spots, take_both, 0)
    for which in range(3):
        frame_weight(which).wait()
        part = jnp.dot(normed[...], w_frame[which], preferred_element_type=jnp.float32)
        if which == 0:
            frame_q[...] = (part * SCORE_SCALE).astype(jnp.bfloat16).T
        elif which == 1:
            frame_k[...] = part.astype(jnp.bfloat16)
        else:
            frame_v[...] = part.astype(jnp.bfloat16).T

    view_rows = spots * rows
    low = lax.broadcasted_iota(jnp.int32, (view_rows, LANES), 1) < head
    ones = jnp.ones((SUM_ROWS, view_rows), jnp.bfloat16)

    def frame_score(i):
        at = slice(i // 2 * LANES, (i // 2 + 1) * LANES)
        mask = jnp.logical_not(low) if i % 2 else low
        return jnp.dot(
            jnp.where(mask, frame_k[:, at], 0), frame_q[at, :],
            preferred_element_type=jnp.float32,
        )

    scores = frame_score(0)
    for i in range(2 * pairs):
        following = frame_score(i + 1) if i + 1 < 2 * pairs else None
        terms = jnp.exp2(scores - jnp.max(scores, axis=0, keepdims=True)).astype(jnp.bfloat16)
        its_values = jnp.concatenate([frame_v[i * head : (i + 1) * head, :], ones], axis=0)
        total = jnp.dot(its_values, terms, preferred_element_type=jnp.float32)
        mixed = (total[:head] / total[head : head + 1]).astype(jnp.bfloat16)
        for j in range(shares):
            mixed_buf[j, i] = mixed[:, j * width : (j + 1) * width]
        scores = following
        if i % 2:
            for step in range(1, shares):
                mixed_copy(i // 2, step).start()
            mixed_own(i // 2).start()

    for pair in range(pairs):
        for j in range(shares):
            arrive(mixed_in.at[j, pl.ds(2 * pair, 2)], mixed_recv.at[pair, j])
    gathered = mixed_in[...].reshape(model_dim, width)
    back_weight().wait()
    added = lax.dot_general(
        gathered, w_back[...], (((0,), (0,)), ((), ())), preferred_element_type=jnp.float32
    )
    stream = raw[pl.ds(share * views_here, views_here)].reshape(width, model_dim)
    after = (stream.astype(jnp.float32) + added).astype(jnp.bfloat16)
    after_buf[...] = after.reshape(views_here, rows, model_dim)
    normed[:width, :] = normalize(after)

    def project(which, stage):
        to_plane = lax.rem(plane + stage, planes)
        part = jnp.dot(
            normed[:width, :], w_global[which * planes + to_plane],
            preferred_element_type=jnp.float32,
        )
        if which == 0:
            part = part * SCORE_SCALE
        part = part.astype(jnp.bfloat16).T
        for i in range(per_plane):
            packed[to_plane * per_plane + i, which] = part[i * head : (i + 1) * head]

    def start_stage(make, stage):
        for step in range(per_plane):
            make(stage, step).start()

    def nth(i):
        odd = lax.rem(i, 2)
        return odd * ((i + 1) // 2) + (1 - odd) * lax.rem(planes - i // 2, planes)

    for i in range(w_global.shape[0]):
        global_weight(i).wait()

    def project_keys(i, carry):
        project(1, nth(i))
        project(2, nth(i))
        return carry

    def project_queries(i, carry):
        project(0, nth(i))
        return carry

    project_queries(1, 0)
    start_stage(q_copy, nth(1))
    project_keys(0, 0)
    for step in range(1, per_plane):
        kv_copy(0, step).start()
    pltpu.make_async_copy(
        packed.at[my_head, pl.ds(1, 2)], got_kv.at[0, spot], kv_recv.at[spot]
    ).start()
    project_keys(1, 0)
    start_stage(kv_copy, nth(1))
    project_queries(0, 0)
    for step in range(1, per_plane):
        q_copy(0, step).start()
    pltpu.make_async_copy(packed.at[my_head, 0], got_q.at[spot], q_recv.at[spot]).start()
    lax.fori_loop(2, planes, project_queries, 0)
    lax.fori_loop(2, planes, project_keys, 0)
    for i in range(2, planes):
        start_stage(q_copy, nth(i))

    def hand_on(stage):
        for i in range(per_plane):
            slot = stage * per_plane + i
            arrive(got_kv.at[0, slot], kv_recv.at[slot])
            for hop in range(1, copies):
                on_copy(slot, hop).start()

    def send_back(block):
        for i in range(per_plane):
            for t in range(views_here):
                either(*back_copy(block, i, t))

    hand_on(0)

    def attend(stage, blocks):
        queries = jnp.concatenate(
            [got_q[block * per_plane + i] for block in blocks for i in range(per_plane)], axis=1
        )
        peak = jnp.concatenate([peaks[block] for block in blocks], axis=1)
        accum = jnp.concatenate([accums[block] for block in blocks], axis=1)
        key_rows = keys.shape[1]
        key_step = min(KEY_STEP, key_rows)

        def score(start):
            return jnp.dot(
                keys[stage, start : start + key_step, :], queries,
                preferred_element_type=jnp.float32,
            )

        def weigh(start, terms):
            return jnp.dot(
                values[stage, :, start : start + key_step], terms,
                preferred_element_type=jnp.float32,
            )

        scores, waiting = score(0), None
        for start in range(0, key_rows, key_step):
            following = score(start + key_step) if start + key_step < key_rows else None
            peak_new = jnp.maximum(peak, jnp.max(scores, axis=0, keepdims=True))
            terms = jnp.exp2(scores - peak_new).astype(jnp.bfloat16)
            fade = jnp.exp2(peak - peak_new)
            if len(blocks) == 1:
                if waiting is not None:
                    accum = accum * waiting[0] + weigh(start - key_step, waiting[1])
                waiting = fade, terms
            else:
                accum = accum * fade + weigh(start, terms)
            peak, scores = peak_new, following
        if waiting is not None:
            accum = accum * waiting[0] + weigh(key_rows - key_step, waiting[1])
        for m, block in enumerate(blocks):
            peaks[block] = peak[:, m * stage_rows : (m + 1) * stage_rows]
            accums[block] = accum[:, m * stage_rows : (m + 1) * stage_rows]

    def lay_keys(stage):
        for hop in range(1, copies):
            for i in range(per_plane):
                slot = stage * per_plane + i
                arrive(got_kv.at[hop, slot], on_recv.at[hop - 1, slot])
        for hop in range(copies):
            for i in range(per_plane):
                slot = stage * per_plane + i
                at = (hop * per_plane + i) * width
                keys[stage, at : at + width, :] = got_kv[hop, slot, 0].T
                values[stage, :head, at : at + width] = got_kv[hop, slot, 1]

    def step_fn(step, carry):
        early = step < 2 * turns
        nth_stage = jnp.where(early, lax.rem(step, 2), step // turns)
        turn = jnp.where(early, step // 2, lax.rem(step, turns))
        first = jnp.where(early, turn == 0, lax.rem(step, turns) == 0)
        stage = nth(nth_stage)
        blocks = [nth(turn * merge + m) for m in range(merge)]

        @pl.when(jnp.logical_and(step >= 1, step + 1 < planes))
        def _():
            start_stage(kv_copy, nth(step + 1))

        @pl.when(first)
        def _():
            lay_keys(stage)

        @pl.when(nth_stage == 0)
        def _():
            for block in blocks:
                for i in range(per_plane):
                    slot = block * per_plane + i
                    arrive(got_q.at[slot], q_recv.at[slot])

        coming = (step + 1) // turns

        @pl.when(jnp.logical_and(lax.rem(step + 1, turns) == 0, coming >= 2))
        def _():
            hand_on(nth(coming))

        @pl.when(step == (planes - 1) * turns - 1)
        def _():
            for t in range(views_here):
                either(*after_copy(t))

        attend(stage, blocks)

        @pl.when(step == 0)
        def _():
            hand_on(nth(1))

        return carry

    def last_fn(i, carry):
        block = nth(planes - 1 - i)
        attend(nth(planes - 1), [block])
        total = accums[block]
        mixed = (total[:head] / total[head : head + 1]).astype(jnp.bfloat16)
        for i in range(per_plane):
            for t in range(views_here):
                at = i * width + t * rows
                out_buf[block * per_plane + i, t] = mixed[:, at : at + rows]
        send_back(block)
        return carry

    lax.fori_loop(0, (planes - 1) * turns, step_fn, 0)
    lay_keys(nth(planes - 1))
    lax.fori_loop(0, planes, last_fn, 0)

    for i in range(views_here):
        for k in range(group):
            for to_core in range(CORES):
                left(*token_copy(i, k, to_core))

    for source in range(spots):
        relay_copy(source).wait_send()

    for pair in range(pairs):
        for step in range(1, shares):
            mixed_copy(pair, step).wait_send()
    for t in range(views_here):
        left(*after_copy(t))

    for stage in range(planes):
        for step in range(per_plane):
            if stage or step:
                q_copy(stage, step).wait_send()
                kv_copy(stage, step).wait_send()
    for slot in range(heads):
        for hop in range(1, copies):
            on_copy(slot, hop).wait_send()

    out_weight().wait()
    for i in range(views_here):
        arrive(after_own.at[i], after_recv.at[i])
        for slot in range(heads):
            arrive(out_back.at[slot, i], out_recv.at[slot, i])
    mixed = jnp.concatenate(
        [out_back[:, i].reshape(heads * head, rows) for i in range(views_here)], axis=1
    )
    added = lax.dot_general(
        mixed, w_out[...], (((0,), (0,)), ((), ())), preferred_element_type=jnp.float32
    )
    stream = after_own[...].reshape(width, model_dim).astype(jnp.float32)
    out_ref[...] = (stream + added).astype(jnp.bfloat16).reshape(views_here, rows, model_dim)

    for block in range(planes):
        for i in range(per_plane):
            for t in range(views_here):
                left(*back_copy(block, i, t))


def on_device(tokens, w_qkv_frame, w_out_frame, w_qkv_global, w_out_global):
    views_here, rows, model_dim = tokens.shape
    spots, view_size = lax.axis_size("head"), lax.axis_size("view")
    heads = model_dim // HEAD
    copies = view_size * spots // heads
    planes = view_size // copies
    group = spots // (CORES * views_here)
    shares = CORES * group
    cols = model_dim // shares
    pairs = cols // LANES
    width = views_here * rows
    per_plane = heads // planes
    stage_rows = per_plane * width
    hops = max(1, copies - 1)
    dma = pltpu.SemaphoreType.DMA
    vmem = lambda *shape: pltpu.VMEM(shape, jnp.bfloat16)
    flops = 4 * heads * view_size * spots * width * width * HEAD
    return pl.pallas_call(
        functools.partial(block_kernel, planes, copies),
        in_specs=[pl.BlockSpec(memory_space=pl.ANY)] * 5,
        out_specs=pl.BlockSpec(memory_space=pltpu.VMEM),
        out_shape=jax.ShapeDtypeStruct(tokens.shape, jnp.bfloat16),
        scratch_shapes=[
            vmem(spots, rows, model_dim),
            vmem(spots * rows, model_dim),
            vmem(3, model_dim, cols),
            vmem(model_dim, model_dim),
            vmem(3 * planes, model_dim, per_plane * HEAD),
            vmem(model_dim, model_dim),
            vmem(cols, spots * rows),
            vmem(spots * rows, cols),
            vmem(cols, spots * rows),
            vmem(shares, cols // HEAD, HEAD, width),
            vmem(shares, cols // HEAD, HEAD, width),
            vmem(views_here, rows, model_dim),
            vmem(views_here, rows, model_dim),
            vmem(heads, 3, HEAD, width),
            vmem(heads, HEAD, width),
            vmem(copies, heads, 2, HEAD, width),
            vmem(planes, copies * stage_rows, HEAD),
            vmem(planes, HEAD + SUM_ROWS, copies * stage_rows),
            pltpu.VMEM((planes, 1, stage_rows), jnp.float32),
            pltpu.VMEM((planes, HEAD + SUM_ROWS, stage_rows), jnp.float32),
            vmem(heads, views_here, HEAD, rows),
            vmem(heads, views_here, HEAD, rows),
            dma((3,)), dma, dma((3 * planes,)), dma,
            dma((views_here, group, CORES)), dma((spots, CORES)), dma((spots,)),
            dma((pairs, shares)), dma((pairs, shares)), dma((views_here,)), dma((views_here,)),
            dma((heads,)), dma((heads,)), dma((heads,)), dma((heads,)),
            dma((hops, heads)), dma((hops, heads)),
            dma((heads, views_here)), dma((heads, views_here)),
        ],
        compiler_params=pltpu.CompilerParams(
            collective_id=0, has_side_effects=True, vmem_limit_bytes=VMEM_BYTES
        ),
        cost_estimate=pl.CostEstimate(flops=flops, bytes_accessed=0, transcendentals=0),
        name="frame_and_global",
    )(tokens, w_qkv_frame, w_out_frame, w_qkv_global, w_out_global)


def solution(mesh):
    return jax.shard_map(
        on_device,
        mesh=mesh,
        in_specs=(P("view", "head", None), P(), P(), P(), P()),
        out_specs=P("view", "head", None),
        check_vma=False,
    )
```

```python
import functools
import math

import jax
import jax.numpy as jnp
from jax import lax
from jax.experimental import pallas as pl
from jax.experimental.pallas import tpu as pltpu
from jax.sharding import PartitionSpec as P

HEAD = 64
LANES = 128
CORES = 2
SUM_ROWS = 16
KEY_STEP = 512
SCORE_SCALE = HEAD ** (-0.5) * math.log2(math.e)
VMEM_BYTES = 52 * 2**20


def normalize(stream):
    widened = stream.astype(jnp.float32)
    center = jnp.mean(widened, axis=-1, keepdims=True)
    spread = jnp.mean(jnp.square(widened - center), axis=-1, keepdims=True)
    return ((widened - center) * lax.rsqrt(spread + 1e-06)).astype(jnp.bfloat16)


def arrive(ref, sem):
    pltpu.make_async_copy(ref, ref, sem).wait()


def block_kernel(
    planes, copies,
    tokens_ref, w_qkv_frame_ref, w_out_frame_ref, w_qkv_global_ref,
    out_back, after_own,
    raw, normed, w_frame, w_back, w_global, frame_q, frame_k, frame_v,
    mixed_buf, mixed_in, after_buf, packed,
    got_q, got_kv, keys, values, peaks, accums, out_buf,
    w_frame_sem, w_back_sem, w_global_sem,
    token_send, token_recv, relay_send, mixed_send, mixed_recv, after_send, after_recv,
    q_send, q_recv, kv_send, kv_recv, on_send, on_recv, out_send, out_recv,
):
    views_here, rows, model_dim = tokens_ref.shape
    view, spot = lax.axis_index("view"), lax.axis_index("head")
    spots, view_size = lax.axis_size("head"), lax.axis_size("view")
    heads, _, head, width = packed.shape
    pairs = mixed_buf.shape[1] // 2
    cols = w_frame.shape[2]
    chunk = w_global.shape[2]
    per_plane = heads // planes
    group = spots // (CORES * views_here)
    shares = CORES * group

    core, row = lax.rem(view, CORES), view // CORES
    mine = spot // group
    share = lax.rem(spot, group) * CORES + core
    first_core, first_local = mine // views_here, lax.rem(mine, views_here)

    plane, copy = view // copies, lax.rem(view, copies)
    my_head = plane * per_plane + spot
    stage_rows = per_plane * width
    half = rows // CORES
    merge = 1 + (planes + 1) % 2
    turns = planes // merge

    def remote(src, dst, send, recv, target):
        return pltpu.make_async_remote_copy(
            src_ref=src, dst_ref=dst, send_sem=send, recv_sem=recv,
            device_id=target, device_id_type=pl.DeviceIdType.MESH,
        )

    def either(here, far, near):
        @pl.when(here)
        def _():
            near().start()

        @pl.when(jnp.logical_not(here))
        def _():
            far().start()

    def left(here, far, near):
        @pl.when(jnp.logical_not(here))
        def _():
            far().wait_send()

    def frame_weight(which):
        at = pl.multiple_of(which * model_dim + share * cols, LANES)
        return pltpu.make_async_copy(
            w_qkv_frame_ref.at[:, pl.ds(at, cols)], w_frame.at[which], w_frame_sem.at[which]
        )

    def global_weight(i):
        return pltpu.make_async_copy(
            w_qkv_global_ref.at[:, i * chunk : (i + 1) * chunk], w_global.at[i],
            w_global_sem.at[i],
        )

    def back_weight():
        return pltpu.make_async_copy(w_out_frame_ref, w_back, w_back_sem)

    def token_copy(i, k, to_core):
        to_spot = (core * views_here + i) * group + k
        part = pl.ds(to_core * half, half)
        src, dst = tokens_ref.at[i, part], raw.at[spot, part]
        landed = token_recv.at[spot, to_core]
        here = jnp.logical_and(to_spot == spot, core == to_core)
        far = lambda: remote(
            src, dst, token_send.at[i, k, to_core], landed, (row * CORES + to_core, to_spot)
        )
        return here, far, lambda: pltpu.make_async_copy(src, dst, landed)

    def relay_copy(source):
        part = raw.at[source, pl.ds(pl.multiple_of(core * half, half), half)]
        return remote(
            part, part, relay_send.at[source], token_recv.at[source, core],
            (row * CORES + (CORES - 1 - core), spot),
        )

    def mixed_copy(pair, step):
        to_share = lax.rem(share + step, shares)
        return remote(
            mixed_buf.at[to_share, pl.ds(2 * pair, 2)], mixed_in.at[share, pl.ds(2 * pair, 2)],
            mixed_send.at[pair, step], mixed_recv.at[pair, share],
            (row * CORES + lax.rem(to_share, CORES), mine * group + to_share // CORES),
        )

    def mixed_own(pair):
        return pltpu.make_async_copy(
            mixed_buf.at[share, pl.ds(2 * pair, 2)], mixed_in.at[share, pl.ds(2 * pair, 2)],
            mixed_recv.at[pair, share],
        )

    def after_copy(t):
        to_view, to_spot = row * CORES + first_core, share * views_here + t
        here = jnp.logical_and(to_view == view, to_spot == spot)
        src, dst, landed = after_buf.at[t], after_own.at[first_local], after_recv.at[first_local]
        far = lambda: remote(src, dst, after_send.at[t], landed, (to_view, to_spot))
        return here, far, lambda: pltpu.make_async_copy(src, dst, landed)

    def device(to_plane, to_spot):
        return (to_plane * copies + copy, to_spot)

    def q_copy(stage, step):
        to_plane, to_spot = lax.rem(plane + stage, planes), lax.rem(spot + step, per_plane)
        slot, order = stage * per_plane + spot, stage * per_plane + step
        return remote(
            packed.at[to_plane * per_plane + to_spot, 0], got_q.at[slot],
            q_send.at[order], q_recv.at[slot], device(to_plane, to_spot),
        )

    def kv_copy(stage, step):
        to_plane, to_spot = lax.rem(plane + stage, planes), lax.rem(spot + step, per_plane)
        slot, order = stage * per_plane + spot, stage * per_plane + step
        return remote(
            packed.at[to_plane * per_plane + to_spot, pl.ds(1, 2)], got_kv.at[0, slot],
            kv_send.at[order], kv_recv.at[slot], device(to_plane, to_spot),
        )

    def on_copy(slot, hop):
        return remote(
            got_kv.at[0, slot], got_kv.at[hop, slot], on_send.at[hop - 1, slot],
            on_recv.at[hop - 1, slot],
            (plane * copies + lax.rem(copy + hop, copies), spot),
        )

    def back_copy(block, i, t):
        slot = block * per_plane + i
        from_view = lax.rem(plane + planes - block, planes) * copies + copy
        from_row, from_core = from_view // CORES, lax.rem(from_view, CORES)
        its_view, its_share = i // group, (i % group) * CORES + from_core
        to_view = from_row * CORES + its_view // views_here
        to_spot = its_share * views_here + t
        here = jnp.logical_and(to_view == view, to_spot == spot)
        src, dst = out_buf.at[slot, t], out_back.at[my_head, its_view % views_here]
        landed = out_recv.at[my_head, its_view % views_here]
        far = lambda: remote(src, dst, out_send.at[slot, t], landed, (to_view, to_spot))
        return here, far, lambda: pltpu.make_async_copy(src, dst, landed)

    for which in range(3):
        frame_weight(which).start()

    barrier = pltpu.get_barrier_semaphore()

    def greet(i, carry):
        pl.semaphore_signal(
            barrier, inc=1,
            device_id=(lax.rem(view + i // spots, view_size), lax.rem(spot + lax.rem(i, spots), spots)),
            device_id_type=pl.DeviceIdType.MESH,
        )
        return carry

    lax.fori_loop(1, view_size * spots, greet, 0)
    pl.semaphore_wait(barrier, view_size * spots - 1)

    for i in range(views_here):
        for k in range(group):
            for to_core in range(CORES):
                either(*token_copy(i, k, to_core))
    back_weight().start()
    for i in range(w_global.shape[0]):
        global_weight(i).start()
    peaks[...] = jnp.full_like(peaks, -1e30)
    accums[...] = jnp.zeros_like(accums)
    values[:, head:, :] = jnp.ones((planes, SUM_ROWS, values.shape[2]), jnp.bfloat16)

    def take(step, its_core):
        source = lax.rem(spot + step, spots)
        part = pl.ds(pl.multiple_of(its_core * half, half), half)
        arrive(raw.at[source, part], token_recv.at[source, its_core])

        @pl.when(its_core == core)
        def _():
            relay_copy(source).start()

        at = pl.ds(pl.multiple_of(source * rows + its_core * half, half), half)
        normed[at, :] = normalize(raw[source, part])

    def take_both(i, carry):
        take(lax.rem(i, spots), lax.rem(core + i // spots, CORES))
        return carry

    lax.fori_loop(0, CORES * spots, take_both, 0)
    for which in range(3):
        frame_weight(which).wait()
        part = jnp.dot(normed[...], w_frame[which], preferred_element_type=jnp.float32)
        if which == 0:
            frame_q[...] = (part * SCORE_SCALE).astype(jnp.bfloat16).T
        elif which == 1:
            frame_k[...] = part.astype(jnp.bfloat16)
        else:
            frame_v[...] = part.astype(jnp.bfloat16).T

    view_rows = spots * rows
    low = lax.broadcasted_iota(jnp.int32, (view_rows, LANES), 1) < head
    ones = jnp.ones((SUM_ROWS, view_rows), jnp.bfloat16)

    def frame_score(i):
        at = slice(i // 2 * LANES, (i // 2 + 1) * LANES)
        mask = jnp.logical_not(low) if i % 2 else low
        return jnp.dot(
            jnp.where(mask, frame_k[:, at], 0), frame_q[at, :],
            preferred_element_type=jnp.float32,
        )

    scores = frame_score(0)
    for i in range(2 * pairs):
        following = frame_score(i + 1) if i + 1 < 2 * pairs else None
        terms = jnp.exp2(scores - jnp.max(scores, axis=0, keepdims=True)).astype(jnp.bfloat16)
        its_values = jnp.concatenate([frame_v[i * head : (i + 1) * head, :], ones], axis=0)
        total = jnp.dot(its_values, terms, preferred_element_type=jnp.float32)
        mixed = (total[:head] / total[head : head + 1]).astype(jnp.bfloat16)
        for j in range(shares):
            mixed_buf[j, i] = mixed[:, j * width : (j + 1) * width]
        scores = following
        if i % 2:
            for step in range(1, shares):
                mixed_copy(i // 2, step).start()
            mixed_own(i // 2).start()

    for pair in range(pairs):
        for j in range(shares):
            arrive(mixed_in.at[j, pl.ds(2 * pair, 2)], mixed_recv.at[pair, j])
    gathered = mixed_in[...].reshape(model_dim, width)
    back_weight().wait()
    added = lax.dot_general(
        gathered, w_back[...], (((0,), (0,)), ((), ())), preferred_element_type=jnp.float32
    )
    stream = raw[pl.ds(share * views_here, views_here)].reshape(width, model_dim)
    after = (stream.astype(jnp.float32) + added).astype(jnp.bfloat16)
    after_buf[...] = after.reshape(views_here, rows, model_dim)
    normed[:width, :] = normalize(after)

    def project(which, stage):
        to_plane = lax.rem(plane + stage, planes)
        part = jnp.dot(
            normed[:width, :], w_global[which * planes + to_plane],
            preferred_element_type=jnp.float32,
        )
        if which == 0:
            part = part * SCORE_SCALE
        part = part.astype(jnp.bfloat16).T
        for i in range(per_plane):
            packed[to_plane * per_plane + i, which] = part[i * head : (i + 1) * head]

    def start_stage(make, stage):
        for step in range(per_plane):
            make(stage, step).start()

    def nth(i):
        odd = lax.rem(i, 2)
        return odd * ((i + 1) // 2) + (1 - odd) * lax.rem(planes - i // 2, planes)

    for i in range(w_global.shape[0]):
        global_weight(i).wait()

    def project_keys(i, carry):
        project(1, nth(i))
        project(2, nth(i))
        return carry

    def project_queries(i, carry):
        project(0, nth(i))
        return carry

    project_queries(1, 0)
    start_stage(q_copy, nth(1))
    project_keys(0, 0)
    for step in range(1, per_plane):
        kv_copy(0, step).start()
    pltpu.make_async_copy(
        packed.at[my_head, pl.ds(1, 2)], got_kv.at[0, spot], kv_recv.at[spot]
    ).start()
    project_keys(1, 0)
    start_stage(kv_copy, nth(1))
    project_queries(0, 0)
    for step in range(1, per_plane):
        q_copy(0, step).start()
    pltpu.make_async_copy(packed.at[my_head, 0], got_q.at[spot], q_recv.at[spot]).start()
    lax.fori_loop(2, planes, project_queries, 0)
    lax.fori_loop(2, planes, project_keys, 0)
    for i in range(2, planes):
        start_stage(q_copy, nth(i))

    def hand_on(stage):
        for i in range(per_plane):
            slot = stage * per_plane + i
            arrive(got_kv.at[0, slot], kv_recv.at[slot])
            for hop in range(1, copies):
                on_copy(slot, hop).start()

    def send_back(block):
        for i in range(per_plane):
            for t in range(views_here):
                either(*back_copy(block, i, t))

    hand_on(0)

    def attend(stage, blocks):
        queries = jnp.concatenate(
            [got_q[block * per_plane + i] for block in blocks for i in range(per_plane)], axis=1
        )
        peak = jnp.concatenate([peaks[block] for block in blocks], axis=1)
        accum = jnp.concatenate([accums[block] for block in blocks], axis=1)
        key_rows = keys.shape[1]
        key_step = min(KEY_STEP, key_rows)

        def score(start):
            return jnp.dot(
                keys[stage, start : start + key_step, :], queries,
                preferred_element_type=jnp.float32,
            )

        def weigh(start, terms):
            return jnp.dot(
                values[stage, :, start : start + key_step], terms,
                preferred_element_type=jnp.float32,
            )

        scores, waiting = score(0), None
        for start in range(0, key_rows, key_step):
            following = score(start + key_step) if start + key_step < key_rows else None
            peak_new = jnp.maximum(peak, jnp.max(scores, axis=0, keepdims=True))
            terms = jnp.exp2(scores - peak_new).astype(jnp.bfloat16)
            fade = jnp.exp2(peak - peak_new)
            if len(blocks) == 1:
                if waiting is not None:
                    accum = accum * waiting[0] + weigh(start - key_step, waiting[1])
                waiting = fade, terms
            else:
                accum = accum * fade + weigh(start, terms)
            peak, scores = peak_new, following
        if waiting is not None:
            accum = accum * waiting[0] + weigh(key_rows - key_step, waiting[1])
        for m, block in enumerate(blocks):
            peaks[block] = peak[:, m * stage_rows : (m + 1) * stage_rows]
            accums[block] = accum[:, m * stage_rows : (m + 1) * stage_rows]

    def lay_keys(stage):
        for hop in range(1, copies):
            for i in range(per_plane):
                slot = stage * per_plane + i
                arrive(got_kv.at[hop, slot], on_recv.at[hop - 1, slot])
        for hop in range(copies):
            for i in range(per_plane):
                slot = stage * per_plane + i
                at = (hop * per_plane + i) * width
                keys[stage, at : at + width, :] = got_kv[hop, slot, 0].T
                values[stage, :head, at : at + width] = got_kv[hop, slot, 1]

    def step_fn(step, carry):
        early = step < 2 * turns
        nth_stage = jnp.where(early, lax.rem(step, 2), step // turns)
        turn = jnp.where(early, step // 2, lax.rem(step, turns))
        first = jnp.where(early, turn == 0, lax.rem(step, turns) == 0)
        stage = nth(nth_stage)
        blocks = [nth(turn * merge + m) for m in range(merge)]

        @pl.when(jnp.logical_and(step >= 1, step + 1 < planes))
        def _():
            start_stage(kv_copy, nth(step + 1))

        @pl.when(first)
        def _():
            lay_keys(stage)

        @pl.when(nth_stage == 0)
        def _():
            for block in blocks:
                for i in range(per_plane):
                    slot = block * per_plane + i
                    arrive(got_q.at[slot], q_recv.at[slot])

        coming = (step + 1) // turns

        @pl.when(jnp.logical_and(lax.rem(step + 1, turns) == 0, coming >= 2))
        def _():
            hand_on(nth(coming))

        @pl.when(step == (planes - 1) * turns - 1)
        def _():
            for t in range(views_here):
                either(*after_copy(t))

        attend(stage, blocks)

        @pl.when(step == 0)
        def _():
            hand_on(nth(1))

        return carry

    def last_fn(i, carry):
        block = nth(planes - 1 - i)
        attend(nth(planes - 1), [block])
        total = accums[block]
        mixed = (total[:head] / total[head : head + 1]).astype(jnp.bfloat16)
        for i in range(per_plane):
            for t in range(views_here):
                at = i * width + t * rows
                out_buf[block * per_plane + i, t] = mixed[:, at : at + rows]
        send_back(block)
        return carry

    lax.fori_loop(0, (planes - 1) * turns, step_fn, 0)
    lay_keys(nth(planes - 1))
    lax.fori_loop(0, planes, last_fn, 0)

    for i in range(views_here):
        for k in range(group):
            for to_core in range(CORES):
                left(*token_copy(i, k, to_core))

    for source in range(spots):
        relay_copy(source).wait_send()

    for pair in range(pairs):
        for step in range(1, shares):
            mixed_copy(pair, step).wait_send()
    for t in range(views_here):
        left(*after_copy(t))

    for stage in range(planes):
        for step in range(per_plane):
            if stage or step:
                q_copy(stage, step).wait_send()
                kv_copy(stage, step).wait_send()
    for slot in range(heads):
        for hop in range(1, copies):
            on_copy(slot, hop).wait_send()

    for i in range(views_here):
        arrive(after_own.at[i], after_recv.at[i])
        for slot in range(heads):
            arrive(out_back.at[slot, i], out_recv.at[slot, i])
    for block in range(planes):
        for i in range(per_plane):
            for t in range(views_here):
                left(*back_copy(block, i, t))


def finish_kernel(mixed_ref, after_ref, weight_ref, out_ref):
    views_here, rows, model_dim = after_ref.shape
    mixed = jnp.concatenate(
        [mixed_ref[:, i].reshape(model_dim, rows) for i in range(views_here)], axis=1
    )
    added = lax.dot_general(
        mixed, weight_ref[...], (((0,), (0,)), ((), ())), preferred_element_type=jnp.float32
    )
    stream = after_ref[...].reshape(views_here * rows, model_dim).astype(jnp.float32)
    out_ref[...] = (stream + added).astype(jnp.bfloat16).reshape(out_ref.shape)


def on_device(tokens, w_qkv_frame, w_out_frame, w_qkv_global, w_out_global):
    views_here, rows, model_dim = tokens.shape
    spots, view_size = lax.axis_size("head"), lax.axis_size("view")
    heads = model_dim // HEAD
    copies = view_size * spots // heads
    planes = view_size // copies
    group = spots // (CORES * views_here)
    shares = CORES * group
    cols = model_dim // shares
    pairs = cols // LANES
    width = views_here * rows
    per_plane = heads // planes
    stage_rows = per_plane * width
    hops = max(1, copies - 1)
    dma = pltpu.SemaphoreType.DMA
    vmem = lambda *shape: pltpu.VMEM(shape, jnp.bfloat16)
    flops = 4 * heads * view_size * spots * width * width * HEAD
    mixed, after = pl.pallas_call(
        functools.partial(block_kernel, planes, copies),
        in_specs=[pl.BlockSpec(memory_space=pl.ANY)] * 4,
        out_specs=[pl.BlockSpec(memory_space=pltpu.VMEM)] * 2,
        out_shape=[
            jax.ShapeDtypeStruct((heads, views_here, HEAD, rows), jnp.bfloat16),
            jax.ShapeDtypeStruct(tokens.shape, jnp.bfloat16),
        ],
        scratch_shapes=[
            vmem(spots, rows, model_dim),
            vmem(spots * rows, model_dim),
            vmem(3, model_dim, cols),
            vmem(model_dim, model_dim),
            vmem(3 * planes, model_dim, per_plane * HEAD),
            vmem(cols, spots * rows),
            vmem(spots * rows, cols),
            vmem(cols, spots * rows),
            vmem(shares, cols // HEAD, HEAD, width),
            vmem(shares, cols // HEAD, HEAD, width),
            vmem(views_here, rows, model_dim),
            vmem(heads, 3, HEAD, width),
            vmem(heads, HEAD, width),
            vmem(copies, heads, 2, HEAD, width),
            vmem(planes, copies * stage_rows, HEAD),
            vmem(planes, HEAD + SUM_ROWS, copies * stage_rows),
            pltpu.VMEM((planes, 1, stage_rows), jnp.float32),
            pltpu.VMEM((planes, HEAD + SUM_ROWS, stage_rows), jnp.float32),
            vmem(heads, views_here, HEAD, rows),
            dma((3,)), dma, dma((3 * planes,)),
            dma((views_here, group, CORES)), dma((spots, CORES)), dma((spots,)),
            dma((pairs, shares)), dma((pairs, shares)), dma((views_here,)), dma((views_here,)),
            dma((heads,)), dma((heads,)), dma((heads,)), dma((heads,)),
            dma((hops, heads)), dma((hops, heads)),
            dma((heads, views_here)), dma((heads, views_here)),
        ],
        compiler_params=pltpu.CompilerParams(
            collective_id=0, has_side_effects=True, vmem_limit_bytes=VMEM_BYTES
        ),
        cost_estimate=pl.CostEstimate(flops=flops, bytes_accessed=0, transcendentals=0),
        name="frame_and_global",
    )(tokens, w_qkv_frame, w_out_frame, w_qkv_global)
    return pl.pallas_call(
        finish_kernel,
        in_specs=[pl.BlockSpec(memory_space=pltpu.VMEM)] * 3,
        out_specs=pl.BlockSpec(memory_space=pltpu.VMEM),
        out_shape=jax.ShapeDtypeStruct(tokens.shape, jnp.bfloat16),
        compiler_params=pltpu.CompilerParams(vmem_limit_bytes=16 * 2**20),
        name="finish",
    )(mixed, after, w_out_global)


def solution(mesh):
    return jax.shard_map(
        on_device,
        mesh=mesh,
        in_specs=(P("view", "head", None), P(), P(), P(), P()),
        out_specs=P("view", "head", None),
        check_vma=False,
    )
```
